512 devices in a mesh: op: 16 (over y, core), lsec: 8 (over z), rsec: 4 (over x).
Axes of the slice: x: 4, y: 8, z: 8, core: 2. Of those that a mesh axis runs over, the one named last changes fastest.
Arguments:
- wavefn: float32 [32, 16, 128, 128], P('lsec', 'rsec'), may hold values from -6 to 6
- left_ops: float32 [112, 32, 128, 128], P('op', 'lsec'), may hold values from -0.5 to 0.5
- right_ops: float32 [112, 16, 128, 128], P('op', 'rsec'), may hold values from -0.046875 to 0.046875
- term_shift: int32 [112], P('op'), may hold values from 0 to 1
Outputs:
- sigma: float32 [32, 16, 128, 128], P('lsec', 'rsec', 'op')
The draws below stay inside these ranges and needn't reach their ends.
All inputs are finite; a program needn't handle non-finite values.
Results may differ from the reference program's by a relative error of at most 0.0001.
Values sent between devices are 32-bit elements; how exact they have to be, the bound alone decides.
A program may use at most 64 MiB of HBM per device.

```python
import jax
import jax.numpy as jnp
from jax import lax

S = 128
LSL = 4
RSL = 4
NL = 32
NR = 16
TERMS = 112
N_LSEC = 8
N_RSEC = 4


def with_ends(values, rng, low, largest):
    longest = values.shape.index(max(values.shape))
    spots = []
    for shift in (0, 1):
        where = [jax.random.randint(jax.random.fold_in(rng, axis), (), 0, length) for axis, length in enumerate(values.shape)]
        where[longest] = (where[longest] + shift) % values.shape[longest]
        spots.append(tuple(where))
    return values.at[spots[0]].set(low).at[spots[1]].set(largest)


def shard_levels(own_key, dims, cuts, low, high):
    def one(axis_at, shards_of):
        draws = jax.random.uniform(jax.random.fold_in(jax.random.fold_in(own_key, 6), axis_at), (shards_of,), jnp.float32, low / len(cuts), high / len(cuts))
        return jnp.repeat(jnp.exp(draws), dims[axis_at] // shards_of).reshape((-1,) + (1,) * (len(dims) - axis_at - 1))

    loudness = one(*cuts[0])
    for cut in cuts[1:]:
        loudness = loudness * one(*cut)
    return loudness


def noise(own_key, dims, scale, reach, pieces=(), dtype=jnp.bfloat16):
    loudness = shard_levels(own_key, dims, pieces, -0.22, 0.18) if pieces else 1.0
    drawn = jax.random.normal(own_key, dims, jnp.float32) * scale * loudness
    return jnp.minimum(jnp.maximum(drawn, -reach), reach).astype(dtype)


def setup_inputs(seed: int = 0) -> dict:
    arg_keys = jax.random.split(jax.random.key(seed), 5)
    wavefn = noise(arg_keys[0], (NL, NR, S, S), 1.0, 6.0, ((0, 8), (1, 4)), jnp.float32)
    left_ops = noise(arg_keys[1], (TERMS, NL, S, S), S ** -0.5, 0.5, ((0, 16), (1, 8)), jnp.float32)
    right_ops = noise(arg_keys[2], (TERMS, NR, S, S), (S * TERMS) ** -0.5, 0.046875, ((0, 16), (1, 4)), jnp.float32)
    term_shift = with_ends(jax.random.randint(arg_keys[3], (TERMS,), 0, 2), jax.random.fold_in(arg_keys[3], 1), 0, 1).astype(jnp.int32)
    return dict(wavefn=wavefn, left_ops=left_ops, right_ops=right_ops, term_shift=term_shift)


def reference(wavefn, left_ops, right_ops, term_shift):
    high = lax.Precision.HIGHEST
    lq = jnp.arange(NL)
    rq = jnp.arange(NR)
    lpos = ((lq % N_LSEC) * LSL + lq // N_LSEC).astype(jnp.int32)
    rpos = ((rq % N_RSEC) * RSL + rq // N_RSEC).astype(jnp.int32)
    psi = wavefn[lpos][:, rpos]
    lop = left_ops[:, lpos]
    rop = right_ops[:, rpos]

    def one_term(carry, items):
        lblock, rblock, shift_bit = items
        inner = jnp.einsum('lij,lrjk->lrik', lblock, psi, precision=high)
        term_out = jnp.einsum('lrik,rmk->lrim', inner, rblock, precision=high)
        weight = shift_bit.astype(jnp.float32)
        return (carry[0] + weight * term_out, carry[1] + (1.0 - weight) * term_out), None

    zero = jnp.zeros((NL, NR, S, S), jnp.float32)
    (rising, falling), _ = lax.scan(one_term, (zero, zero), (lop, rop, term_shift))
    moved = jnp.zeros((NL, NR, S, S), jnp.float32)
    moved = moved.at[1:, :-1].add(rising[:-1, 1:])
    moved = moved.at[:-1, 1:].add(falling[1:, :-1])
    lp = jnp.arange(NL)
    rp = jnp.arange(NR)
    lsec_of = ((lp % LSL) * N_LSEC + lp // LSL).astype(jnp.int32)
    rsec_of = ((rp % RSL) * N_RSEC + rp // RSL).astype(jnp.int32)
    return moved[lsec_of][:, rsec_of]
```

```python
import jax
import jax.numpy as jnp
from jax import lax
from jax.experimental import pallas as pl
from jax.experimental.pallas import tpu as pltpu
from jax.sharding import PartitionSpec as P

MESH = pl.DeviceIdType.MESH
F32 = jnp.float32
BF16 = jnp.bfloat16


def split(value):
    high = value.astype(BF16)
    return high, (value - high.astype(F32)).astype(BF16)


def kernel(shift, psi, lop, rop, out, lcat, pcat, wcat, wlow, x, acc, peer, ring, moved, send, recv):
    terms, nl = lop.shape[0], lop.shape[1]
    nr = psi.shape[1]
    s = psi.shape[2]
    ny = lop.shape[2]
    half = s // 2
    depth = terms * s

    op = lax.axis_index("op")
    lsec = lax.axis_index("lsec")
    rsec = lax.axis_index("rsec")
    n_lsec, n_rsec = lax.axis_size("lsec"), lax.axis_size("rsec")
    y, core = op // 2, op % 2
    partner = {"op": y * 2 + (1 - core)}
    ahead = {"op": ((y + 1) % ny) * 2 + core}
    behind = {"op": ((y + ny - 1) % ny) * 2 + core}
    raise_to = {"lsec": (lsec + 1) % n_lsec, "rsec": (rsec + n_rsec - 1) % n_rsec}
    lower_to = {"lsec": (lsec + n_lsec - 1) % n_lsec, "rsec": (rsec + 1) % n_rsec}

    barrier = pltpu.get_barrier_semaphore()
    for who in (partner, ahead, behind, raise_to, lower_to):
        pl.semaphore_signal(barrier, inc=1, device_id=who, device_id_type=MESH)

    for l in range(nl):
        for t in range(terms):
            for h in range(2):
                c = (1 - core) if h == 0 else core
                high, low = split(lop[t, l, :, c].reshape(half, s))
                rows = pl.ds((t * 2 + h) * half, half)
                lcat[l, rows, 0:s] = high
                lcat[l, rows, s : 2 * s] = low

    for r in range(nr):
        for t in range(terms):
            weight = shift[t].astype(F32)
            for k, w in enumerate((weight, 1.0 - weight)):
                high, low = split(rop[t, r] * w)
                rows = pl.ds(k * s, s)
                wcat[r, rows, t * s : (t + 1) * s] = high
                wcat[r, rows, depth + t * s : depth + (t + 1) * s] = high
                wlow[r, rows, t * s : (t + 1) * s] = low

    def remote(src, dst, n, r, who):
        return pltpu.make_async_remote_copy(
            src_ref=src, dst_ref=dst, send_sem=send.at[r, n], recv_sem=recv.at[r, n], device_id=who, device_id_type=MESH
        )

    def chunk(r, far, k=None):
        at = acc.at[r, 1, :, (y + far + ny) % ny]
        return at if k is None else at.at[:, :, pl.ds(k * s, s)]

    pending = []

    def exchange(r):
        return remote(acc.at[r, 0], peer.at[r], 0, r, partner)

    def ring_copy(r, d, step):
        far = (4 - step) if d == 0 else (step - 4)
        who = ahead if d == 0 else behind
        n = 1 + d * 4 + step
        if step == 0:
            return remote(chunk(r, far, d), ring.at[r, d, step, :, :, pl.ds(d * s, s)], n, r, who)
        return remote(chunk(r, far), ring.at[r, d, step], n, r, who)

    def move_copy(r, k):
        who = raise_to if k == 0 else lower_to
        return remote(chunk(r, 0, k), moved.at[k, :, r], 9 + k, r, who)

    def multiply(r):
        for l in range(nl):
            high, low = split(psi[l, r])
            for k in range(2):
                pcat[l, k * s : (k + 1) * s, 0:s] = high
                pcat[l, k * s : (k + 1) * s, s : 2 * s] = low
        for l in range(nl):
            both = jnp.dot(lcat[l], pcat[l], preferred_element_type=F32)
            high, low = split(both[:, 0:s] + both[:, s : 2 * s])
            for t in range(terms):
                for h in range(2):
                    rows = slice((t * 2 + h) * half, (t * 2 + h + 1) * half)
                    at = pl.ds(h * nl * half + l * half, half)
                    x[at, t * s : (t + 1) * s] = high[rows]
                    x[at, depth + t * s : depth + (t + 1) * s] = low[rows]
        nt = (((1,), (1,)), ((), ()))
        total = lax.dot_general(x[...], wcat[r], nt, preferred_element_type=F32)
        total += lax.dot_general(x[:, 0:depth], wlow[r], nt, preferred_element_type=F32)
        acc[r] = total.reshape(2, nl, ny, 8, 2 * s)

    for r in range(nr):
        multiply(r)
    pl.semaphore_wait(barrier, 5)
    for r in range(nr):
        exchange(r).start()
    for r in range(nr):
        exchange(r).wait_recv()
        acc[r, 1] += peer[r]
        for d in range(2):
            ring_copy(r, d, 0).start()
    for step in range(4):
        for r in range(nr):
            for d in range(2):
                ring_copy(r, d, step).wait_recv()
                far = (3 - step) if d == 0 else (step - 3)
                at = (y + far + ny) % ny
                if step == 0:
                    lanes = pl.ds(d * s, s)
                    acc[r, 1, :, at, :, lanes] += ring[r, d, step, :, :, lanes]
                else:
                    acc[r, 1, :, at] += ring[r, d, step]
                if step < 3:
                    ring_copy(r, d, step + 1).start()
            if step == 3:
                for k in range(2):
                    move_copy(r, k).start()
    for r in range(nr):
        for k in range(2):
            move_copy(r, k).wait_recv()

    up_l = (lsec == 0).astype(jnp.int32)
    up_r = (rsec == n_rsec - 1).astype(jnp.int32)
    down_l = (lsec == n_lsec - 1).astype(jnp.int32)
    down_r = (rsec == 0).astype(jnp.int32)

    def picked(k, l, r):
        inside = (l >= 0) & (l < nl) & (r >= 0) & (r < nr)
        tile = moved[k, jnp.clip(l, 0, nl - 1), jnp.clip(r, 0, nr - 1)]
        return jnp.where(inside, tile, 0.0)

    for l in range(nl):
        for r in range(nr):
            out[l, r] = picked(0, l - up_l, r + up_r) + picked(1, l + down_l, r - down_r)

    for r in range(nr):
        exchange(r).wait_send()
        for d in range(2):
            for step in range(4):
                ring_copy(r, d, step).wait_send()
        for k in range(2):
            move_copy(r, k).wait_send()


def shards(wavefn, left_ops, right_ops, term_shift):
    nl, nr, s = wavefn.shape[:3]
    terms = left_ops.shape[0]
    ny = lax.axis_size("op") // 2
    vmem = pl.BlockSpec(memory_space=pltpu.VMEM)
    return pl.pallas_call(
        kernel,
        out_shape=jax.ShapeDtypeStruct((nl, nr, s // (2 * ny), s), F32),
        in_specs=[pl.BlockSpec(memory_space=pltpu.SMEM), vmem, vmem, vmem],
        out_specs=vmem,
        scratch_shapes=[
            pltpu.VMEM((nl, terms * s, 2 * s), BF16),
            pltpu.VMEM((nl, 2 * s, 2 * s), BF16),
            pltpu.VMEM((nr, 2 * s, 2 * terms * s), BF16),
            pltpu.VMEM((nr, 2 * s, terms * s), BF16),
            pltpu.VMEM((nl * s, 2 * terms * s), BF16),
            pltpu.VMEM((nr, 2, nl, ny, 8, 2 * s), F32),
            pltpu.VMEM((nr, nl, ny, 8, 2 * s), F32),
            pltpu.VMEM((nr, 2, 4, nl, 8, 2 * s), F32),
            pltpu.VMEM((2, nl, nr, 8, s), F32),
            pltpu.SemaphoreType.DMA((nr, 11)),
            pltpu.SemaphoreType.DMA((nr, 11)),
        ],
        compiler_params=pltpu.CompilerParams(collective_id=0, has_side_effects=True, vmem_limit_bytes=60 * 2**20),
        name="sigma",
    )(term_shift, wavefn, left_ops.reshape(terms, nl, ny, 2, 8, s), right_ops)


def solution(mesh):
    placed = (
        P("lsec", "rsec", None, None),
        P("op", "lsec", None, None),
        P("op", "rsec", None, None),
        P("op"),
    )
    return jax.shard_map(
        shards, mesh=mesh, in_specs=placed, out_specs=P("lsec", "rsec", "op", None), check_vma=False
    )
```

```python
import jax
import jax.numpy as jnp
from jax import lax
from jax.experimental import pallas as pl
from jax.experimental.pallas import tpu as pltpu
from jax.sharding import PartitionSpec as P

MESH = pl.DeviceIdType.MESH
F32 = jnp.float32
BF16 = jnp.bfloat16
FAR = (4, 3, -3, 2, -2, 1, -1, 0)
GROUPS = ((0, 5), (5, 8))
NEAR = (0, 1, -1)
SLOT = {far: at for at, far in enumerate(FAR)}


def split(value):
    high = value.astype(BF16)
    return high, (value - high.astype(F32)).astype(BF16)


def kernel(
    shift, psi_hbm, lop_hbm, rop_hbm, out,
    psi, lop, rop, lcat, pcat, wcat, wlow, x, acc, peer, ring, final, load, send, recv,
):
    terms, nl, ny = lop.shape[0], lop.shape[1], lop.shape[2]
    nr, s = psi.shape[1], psi.shape[2]
    depth = terms * s

    op = lax.axis_index("op")
    lsec = lax.axis_index("lsec")
    rsec = lax.axis_index("rsec")
    n_lsec, n_rsec = lax.axis_size("lsec"), lax.axis_size("rsec")
    y, core = op // 2, op % 2

    def along(steps):
        return ((y + steps + ny) % ny) * 2 + core

    partner = {"op": y * 2 + (1 - core)}
    ring_to = {steps: {"op": along(steps)} for steps in (1, -1, 2, -2)}
    first_class = ((lsec > 0) & (lsec < n_lsec - 1)).astype(jnp.int32)
    classes = (first_class, 1 - first_class)

    def final_to(k, steps):
        sign = 1 - 2 * k
        return {
            "op": along(steps),
            "lsec": (lsec + sign + n_lsec) % n_lsec,
            "rsec": (rsec - sign + n_rsec) % n_rsec,
        }

    loads = []
    for l in range(nl):
        loads.append((psi_hbm.at[l], psi.at[l]))
        loads.append((lop_hbm.at[:, l], lop.at[:, l]))
    for r in range(nr):
        loads.append((rop_hbm.at[:, r], rop.at[:, r]))
    loads = [pltpu.make_async_copy(src, dst, load.at[i]) for i, (src, dst) in enumerate(loads)]
    for copy in loads:
        copy.start()

    barrier = pltpu.get_barrier_semaphore()
    greeted = [partner, *ring_to.values(), *(final_to(k, steps) for k in range(2) for steps in NEAR)]
    for who in greeted:
        pl.semaphore_signal(barrier, inc=1, device_id=who, device_id_type=MESH)

    sent = []

    def remote(src, dst, n, r, who):
        return pltpu.make_async_remote_copy(
            src_ref=src, dst_ref=dst, send_sem=send.at[r, n], recv_sem=recv.at[r, n], device_id=who, device_id_type=MESH
        )

    def start(copy):
        copy.start()
        sent.append(copy)

    def exchange(r, g):
        slots = pl.ds(GROUPS[g][0], GROUPS[g][1] - GROUPS[g][0])
        return remote(acc.at[r, 1 - core, slots], peer.at[r, slots], g, r, partner)

    def relays(r, stage):
        if stage == 0:
            return ((3, 1, 2), (-3, -1, -2), (4, 2, 2) if r % 2 == 0 else (4, -2, -2))
        return ((2, 1, 1), (-2, -1, -1))

    def relay_copy(r, k, stage, at):
        far, steps, _ = relays(r, stage)[at]
        n = 3 * stage + at
        return remote(acc.at[r, core, SLOT[far], k], ring.at[r, k, n], 2 + k * 5 + n, r, ring_to[steps])

    def start_relays(r, k, stage):
        for at in range(3 - stage):
            start(relay_copy(r, k, stage, at))

    def final_copy(r, k, at):
        far = NEAR[at]
        return remote(acc.at[r, core, SLOT[far], k], final.at[k, at, r], 12 + k * 3 + at, r, final_to(k, far))

    def split_left(g, l):
        first, last = GROUPS[g]
        for t in range(terms):
            for at in range(first, last):
                high, low = split(lop[t, l, (y + FAR[at] + ny) % ny])
                rows = pl.ds((t * (last - first) + at - first) * 16, 16)
                lcat[l, rows, 0:s] = high
                lcat[l, rows, s : 2 * s] = low

    def split_wave(l):
        for r in range(nr):
            high, low = split(psi[l, r])
            for k in range(2):
                pcat[l, r, k * s : (k + 1) * s, 0:s] = high
                pcat[l, r, k * s : (k + 1) * s, s : 2 * s] = low

    def split_right(r):
        for t in range(terms):
            weight = shift[t].astype(F32)
            for k, w in enumerate((weight, 1.0 - weight)):
                high, low = split(rop[t, r] * w)
                rows = pl.ds(k * s, s)
                wcat[r, rows, t * s : (t + 1) * s] = high
                wcat[r, rows, depth + t * s : depth + (t + 1) * s] = high
                wlow[r, rows, t * s : (t + 1) * s] = low

    def first_product(g, l, r):
        first, last = GROUPS[g]
        size = (last - first) * 16
        both = jnp.dot(lcat[l, 0 : terms * size], pcat[l, r], preferred_element_type=F32)
        high, low = split(both[:, 0:s] + both[:, s : 2 * s])
        rows = pl.ds(l * size, size)
        for t in range(terms):
            x[r, rows, t * s : (t + 1) * s] = high[t * size : (t + 1) * size]
            x[r, rows, depth + t * s : depth + (t + 1) * s] = low[t * size : (t + 1) * size]

    def second_product(g, r):
        first, last = GROUPS[g]
        size = (last - first) * 16
        nt = (((1,), (1,)), ((), ()))
        total = lax.dot_general(x[r, 0 : nl * size], wcat[r], nt, preferred_element_type=F32)
        total += lax.dot_general(x[r, 0 : nl * size, 0:depth], wlow[r], nt, preferred_element_type=F32)
        total = total.reshape(nl, last - first, 2, 8, 2 * s)
        for l in range(nl):
            for c in range(2):
                for k in range(2):
                    acc[r, c, first:last, k, l] = total[l, :, c, :, k * s : (k + 1) * s]

    def take_exchange(g, r):
        first, last = GROUPS[g]
        exchange(r, g).wait_recv()
        acc[r, core, first:last] += peer[r, first:last]

    def take_relays(r, k, stage):
        for at in range(3 - stage):
            relay_copy(r, k, stage, at).wait_recv()
        for at in range(3 - stage):
            far = relays(r, stage)[at][2]
            acc[r, core, SLOT[far], k] += ring[r, k, 3 * stage + at]

    for l in range(nl):
        loads[2 * l].wait()
        loads[2 * l + 1].wait()
        split_wave(l)
        split_left(0, l)
        for r in range(nr):
            first_product(0, l, r)
    for r in range(nr):
        loads[2 * nl + r].wait()
        split_right(r)
        second_product(0, r)
        if r == 0:
            pl.semaphore_wait(barrier, len(greeted))
        start(exchange(r, 0))
    for r in range(nr):
        take_exchange(0, r)
        start_relays(r, classes[0], 0)
    for r in range(nr):
        start_relays(r, classes[1], 0)
    for l in range(nl):
        split_left(1, l)
        for r in range(nr):
            first_product(1, l, r)
    for r in range(nr):
        second_product(1, r)
        start(exchange(r, 1))
    for k in classes:
        for r in range(nr):
            take_relays(r, k, 0)
            start_relays(r, k, 1)
    for r in range(nr):
        take_exchange(1, r)
        start(final_copy(r, classes[0], 0))
    for k in classes:
        for r in range(nr):
            take_relays(r, k, 1)
            for at in range(1, 3):
                start(final_copy(r, k, at))
        if k is classes[0]:
            for r in range(nr):
                start(final_copy(r, classes[1], 0))

    up_l = (lsec == 0).astype(jnp.int32)
    up_r = (rsec == n_rsec - 1).astype(jnp.int32)
    down_l = (lsec == n_lsec - 1).astype(jnp.int32)
    down_r = (rsec == 0).astype(jnp.int32)

    def picked(k, l, r):
        inside = (l >= 0) & (l < nl) & (r >= 0) & (r < nr)
        l, r = jnp.clip(l, 0, nl - 1), jnp.clip(r, 0, nr - 1)
        tile = sum(final[k, at, r, l] for at in range(1, len(NEAR))) + final[k, 0, r, l]
        return jnp.where(inside, tile, 0.0)

    for r in range(nr):
        for at in range(len(NEAR)):
            for k in range(2):
                final_copy(r, k, at).wait_recv()
    for l in range(nl):
        for r in range(nr):
            out[l, r] = picked(0, l - up_l, r + up_r) + picked(1, l + down_l, r - down_r)
    for copy in sent:
        copy.wait_send()


def shards(wavefn, left_ops, right_ops, term_shift):
    nl, nr, s = wavefn.shape[:3]
    terms = left_ops.shape[0]
    ny = lax.axis_size("op") // 2
    most = max(last - first for first, last in GROUPS) * 16
    hbm = pl.BlockSpec(memory_space=pl.ANY)
    left_ops = left_ops.reshape(terms, nl, ny, 16, s)
    return pl.pallas_call(
        kernel,
        out_shape=jax.ShapeDtypeStruct((nl, nr, 8, s), F32),
        in_specs=[pl.BlockSpec(memory_space=pltpu.SMEM), hbm, hbm, hbm],
        out_specs=pl.BlockSpec(memory_space=pltpu.VMEM),
        scratch_shapes=[
            pltpu.VMEM(wavefn.shape, F32),
            pltpu.VMEM(left_ops.shape, F32),
            pltpu.VMEM(right_ops.shape, F32),
            pltpu.VMEM((nl, terms * most, 2 * s), BF16),
            pltpu.VMEM((nl, nr, 2 * s, 2 * s), BF16),
            pltpu.VMEM((nr, 2 * s, 2 * terms * s), BF16),
            pltpu.VMEM((nr, 2 * s, terms * s), BF16),
            pltpu.VMEM((nr, nl * most, 2 * terms * s), BF16),
            pltpu.VMEM((nr, 2, ny, 2, nl, 8, s), F32),
            pltpu.VMEM((nr, ny, 2, nl, 8, s), F32),
            pltpu.VMEM((nr, 2, 5, nl, 8, s), F32),
            pltpu.VMEM((2, len(NEAR), nr, nl, 8, s), F32),
            pltpu.SemaphoreType.DMA((2 * nl + nr,)),
            pltpu.SemaphoreType.DMA((nr, 18)),
            pltpu.SemaphoreType.DMA((nr, 18)),
        ],
        compiler_params=pltpu.CompilerParams(collective_id=0, has_side_effects=True, vmem_limit_bytes=60 * 2**20),
        name="sigma",
    )(term_shift, wavefn, left_ops, right_ops)


def solution(mesh):
    placed = (
        P("lsec", "rsec", None, None),
        P("op", "lsec", None, None),
        P("op", "rsec", None, None),
        P("op"),
    )
    return jax.shard_map(
        shards, mesh=mesh, in_specs=placed, out_specs=P("lsec", "rsec", "op", None), check_vma=False
    )
```

```python
import jax
import jax.numpy as jnp
from jax import lax
from jax.experimental import pallas as pl
from jax.experimental.pallas import tpu as pltpu
from jax.sharding import PartitionSpec as P

MESH = pl.DeviceIdType.MESH
F32 = jnp.float32
BF16 = jnp.bfloat16
FAR = (4, 3, -3, 2, -2, 1, -1, 0)
GROUPS = ((0, 5), (5, 8))
NEAR = (0, 1, -1)
SLOT = {far: at for at, far in enumerate(FAR)}


def split(value):
    high = value.astype(BF16)
    return high, (value - high.astype(F32)).astype(BF16)


def kernel(
    shift, psi_hbm, lop_hbm, rop_hbm, out,
    psi, lop, rop, lcat, pcat, wcat, wlow, x, acc, peer, ring, final, load, send, recv,
):
    terms, nl, ny = lop.shape[0], lop.shape[1], lop.shape[2]
    nr, s = psi.shape[1], psi.shape[2]
    depth = terms * s

    op = lax.axis_index("op")
    lsec = lax.axis_index("lsec")
    rsec = lax.axis_index("rsec")
    n_lsec, n_rsec = lax.axis_size("lsec"), lax.axis_size("rsec")
    y, core = op // 2, op % 2

    def along(steps):
        return ((y + steps + ny) % ny) * 2 + core

    partner = {"op": y * 2 + (1 - core)}
    ring_to = {steps: {"op": along(steps)} for steps in (1, -1, 2, -2)}
    first_class = ((lsec > 0) & (lsec < n_lsec - 1)).astype(jnp.int32)
    classes = (first_class, 1 - first_class)

    def final_to(k, steps):
        sign = 1 - 2 * k
        return {
            "op": along(steps),
            "lsec": (lsec + sign + n_lsec) % n_lsec,
            "rsec": (rsec - sign + n_rsec) % n_rsec,
        }

    loads = []
    for l in range(nl):
        loads.append((psi_hbm.at[l], psi.at[l]))
        loads.append((lop_hbm.at[:, l], lop.at[:, l]))
    for r in range(nr):
        loads.append((rop_hbm.at[:, r], rop.at[:, r]))
    loads = [pltpu.make_async_copy(src, dst, load.at[i]) for i, (src, dst) in enumerate(loads)]
    for copy in loads:
        copy.start()

    barrier = pltpu.get_barrier_semaphore()
    greeted = [partner, *ring_to.values(), *(final_to(k, steps) for k in range(2) for steps in NEAR)]
    for who in greeted:
        pl.semaphore_signal(barrier, inc=1, device_id=who, device_id_type=MESH)

    sent = []

    def remote(src, dst, n, r, who):
        return pltpu.make_async_remote_copy(
            src_ref=src, dst_ref=dst, send_sem=send.at[r, n], recv_sem=recv.at[r, n], device_id=who, device_id_type=MESH
        )

    def start(copy):
        copy.start()
        sent.append(copy)

    def exchange(r, g):
        slots = pl.ds(GROUPS[g][0], GROUPS[g][1] - GROUPS[g][0])
        return remote(acc.at[r, 1 - core, slots], peer.at[r, slots], g, r, partner)

    def relays(r, stage):
        if stage == 0:
            return ((3, 1, 2), (-3, -1, -2), (4, 2, 2) if r % 2 == 0 else (4, -2, -2))
        return ((2, 1, 1), (-2, -1, -1))

    def relay_copy(r, k, stage, at):
        far, steps, _ = relays(r, stage)[at]
        n = 3 * stage + at
        return remote(acc.at[r, core, SLOT[far], k], ring.at[r, k, n], 2 + k * 5 + n, r, ring_to[steps])

    def start_relays(r, k, stage):
        for at in range(3 - stage):
            start(relay_copy(r, k, stage, at))

    def final_copy(r, k, at):
        far = NEAR[at]
        return remote(acc.at[r, core, SLOT[far], k], final.at[k, at, r], 12 + k * 3 + at, r, final_to(k, far))

    def split_left(g, l):
        first, last = GROUPS[g]
        for t in range(terms):
            for at in range(first, last):
                high, low = split(lop[t, l, (y + FAR[at] + ny) % ny])
                rows = pl.ds((t * (last - first) + at - first) * 16, 16)
                lcat[l, rows, 0:s] = high
                lcat[l, rows, s : 2 * s] = low

    def split_wave(l):
        for r in range(nr):
            high, low = split(psi[l, r])
            for k in range(2):
                pcat[l, r, k * s : (k + 1) * s, 0:s] = high
                pcat[l, r, k * s : (k + 1) * s, s : 2 * s] = low

    def split_right(r):
        for t in range(terms):
            weight = shift[t].astype(F32)
            for k, w in enumerate((weight, 1.0 - weight)):
                high, low = split(rop[t, r] * w)
                rows = pl.ds(k * s, s)
                wcat[r, rows, t * s : (t + 1) * s] = high
                wcat[r, rows, depth + t * s : depth + (t + 1) * s] = high
                wlow[r, rows, t * s : (t + 1) * s] = low

    def first_product(g, l, r):
        first, last = GROUPS[g]
        size = (last - first) * 16
        both = jnp.dot(lcat[l, 0 : terms * size], pcat[l, r], preferred_element_type=F32)
        high, low = split(both[:, 0:s] + both[:, s : 2 * s])
        rows = pl.ds(l * size, size)
        for t in range(terms):
            x[r, rows, t * s : (t + 1) * s] = high[t * size : (t + 1) * size]
            x[r, rows, depth + t * s : depth + (t + 1) * s] = low[t * size : (t + 1) * size]

    def second_product(g, r):
        first, last = GROUPS[g]
        size = (last - first) * 16
        nt = (((1,), (1,)), ((), ()))
        total = lax.dot_general(x[r, 0 : nl * size], wcat[r], nt, preferred_element_type=F32)
        total += lax.dot_general(x[r, 0 : nl * size, 0:depth], wlow[r], nt, preferred_element_type=F32)
        total = total.reshape(nl, last - first, 2, 8, 2 * s)
        for l in range(nl):
            for c in range(2):
                for k in range(2):
                    acc[r, c, first:last, k, l] = total[l, :, c, :, k * s : (k + 1) * s]

    def take_exchange(g, r):
        first, last = GROUPS[g]
        exchange(r, g).wait_recv()
        acc[r, core, first:last] += peer[r, first:last]

    def take_relays(r, k, stage):
        for at in range(3 - stage):
            relay_copy(r, k, stage, at).wait_recv()
        for at in range(3 - stage):
            far = relays(r, stage)[at][2]
            acc[r, core, SLOT[far], k] += ring[r, k, 3 * stage + at]

    for l in range(nl):
        loads[2 * l].wait()
        loads[2 * l + 1].wait()
        split_wave(l)
        split_left(0, l)
        for r in range(nr):
            first_product(0, l, r)
    for r in range(nr):
        loads[2 * nl + r].wait()
        split_right(r)
        second_product(0, r)
        if r == 0:
            pl.semaphore_wait(barrier, len(greeted))
        start(exchange(r, 0))
    for r in range(nr):
        take_exchange(0, r)
        start_relays(r, classes[0], 0)
    for r in range(nr):
        start_relays(r, classes[1], 0)
    for l in range(nl):
        split_left(1, l)
        for r in range(nr):
            first_product(1, l, r)
    for r in range(nr):
        second_product(1, r)
        start(exchange(r, 1))
    for k in classes:
        for r in range(nr):
            take_relays(r, k, 0)
            start_relays(r, k, 1)
    for r in range(nr):
        take_exchange(1, r)
        start(final_copy(r, classes[0], 0))
    for k in classes:
        for r in range(nr):
            take_relays(r, k, 1)
            for at in range(1, 3):
                start(final_copy(r, k, at))
        if k is classes[0]:
            for r in range(nr):
                start(final_copy(r, classes[1], 0))

    up_l = (lsec == 0).astype(jnp.int32)
    up_r = (rsec == n_rsec - 1).astype(jnp.int32)
    down_l = (lsec == n_lsec - 1).astype(jnp.int32)
    down_r = (rsec == 0).astype(jnp.int32)

    def picked(k, l, r):
        inside = (l >= 0) & (l < nl) & (r >= 0) & (r < nr)
        l, r = jnp.clip(l, 0, nl - 1), jnp.clip(r, 0, nr - 1)
        tile = sum(final[k, at, r, l] for at in range(1, len(NEAR))) + final[k, 0, r, l]
        return jnp.where(inside, tile, 0.0)

    for r in range(nr):
        for at in range(len(NEAR)):
            for k in range(2):
                final_copy(r, k, at).wait_recv()
    for l in range(nl):
        for r in range(nr):
            out[l, r] = picked(0, l - up_l, r + up_r) + picked(1, l + down_l, r - down_r)
    for copy in sent:
        copy.wait_send()


def shards(wavefn, left_ops, right_ops, term_shift):
    nl, nr, s = wavefn.shape[:3]
    terms = left_ops.shape[0]
    ny = lax.axis_size("op") // 2
    most = max(last - first for first, last in GROUPS) * 16
    hbm = pl.BlockSpec(memory_space=pl.ANY)
    left_ops = left_ops.reshape(terms, nl, ny, 16, s)
    return pl.pallas_call(
        kernel,
        out_shape=pltpu.VMEM((nl, nr, 8, s), F32),
        in_specs=[pl.BlockSpec(memory_space=pltpu.SMEM), hbm, hbm, hbm],
        out_specs=pl.BlockSpec(memory_space=pltpu.VMEM),
        scratch_shapes=[
            pltpu.VMEM(wavefn.shape, F32),
            pltpu.VMEM(left_ops.shape, F32),
            pltpu.VMEM(right_ops.shape, F32),
            pltpu.VMEM((nl, terms * most, 2 * s), BF16),
            pltpu.VMEM((nl, nr, 2 * s, 2 * s), BF16),
            pltpu.VMEM((nr, 2 * s, 2 * terms * s), BF16),
            pltpu.VMEM((nr, 2 * s, terms * s), BF16),
            pltpu.VMEM((nr, nl * most, 2 * terms * s), BF16),
            pltpu.VMEM((nr, 2, ny, 2, nl, 8, s), F32),
            pltpu.VMEM((nr, ny, 2, nl, 8, s), F32),
            pltpu.VMEM((nr, 2, 5, nl, 8, s), F32),
            pltpu.VMEM((2, len(NEAR), nr, nl, 8, s), F32),
            pltpu.SemaphoreType.DMA((2 * nl + nr,)),
            pltpu.SemaphoreType.DMA((nr, 18)),
            pltpu.SemaphoreType.DMA((nr, 18)),
        ],
        compiler_params=pltpu.CompilerParams(collective_id=0, has_side_effects=True, vmem_limit_bytes=60 * 2**20),
        name="sigma",
    )(term_shift, wavefn, left_ops, right_ops)


def solution(mesh):
    placed = (
        P("lsec", "rsec", None, None),
        P("op", "lsec", None, None),
        P("op", "rsec", None, None),
        P("op"),
    )
    return jax.shard_map(
        shards, mesh=mesh, in_specs=placed, out_specs=P("lsec", "rsec", "op", None), check_vma=False
    )
```

```python
import jax
import jax.numpy as jnp
from jax import lax
from jax.experimental import pallas as pl
from jax.experimental.pallas import tpu as pltpu
from jax.sharding import PartitionSpec as P

MESH = pl.DeviceIdType.MESH
F32 = jnp.float32
BF16 = jnp.bfloat16
FAR = (4, 3, -3, 2, -2, 1, -1, 0)
GROUPS = ((0, 3), (3, 8))
NEAR = (0, 1, -1)
SLOT = {far: at for at, far in enumerate(FAR)}


def split(value):
    high = value.astype(BF16)
    return high, (value - high.astype(F32)).astype(BF16)


def kernel(
    shift, psi_hbm, lop_hbm, rop_hbm, out,
    psi, lop, rop, lcat, pcat, wcat, wlow, x, acc, peer, ring, final, load, send, recv,
):
    terms, nl, ny = lop.shape[0], lop.shape[1], lop.shape[2]
    nr, s = psi.shape[1], psi.shape[2]
    depth = terms * s

    op = lax.axis_index("op")
    lsec = lax.axis_index("lsec")
    rsec = lax.axis_index("rsec")
    n_lsec, n_rsec = lax.axis_size("lsec"), lax.axis_size("rsec")
    y, core = op // 2, op % 2

    def along(steps):
        return ((y + steps + ny) % ny) * 2 + core

    partner = {"op": y * 2 + (1 - core)}
    ring_to = {steps: {"op": along(steps)} for steps in (1, -1, 2, -2)}
    first_class = ((lsec > 0) & (lsec < n_lsec - 1)).astype(jnp.int32)
    classes = (first_class, 1 - first_class)

    def final_to(k, steps):
        sign = 1 - 2 * k
        return {
            "op": along(steps),
            "lsec": (lsec + sign + n_lsec) % n_lsec,
            "rsec": (rsec - sign + n_rsec) % n_rsec,
        }

    loads = []
    for l in range(nl):
        loads.append((psi_hbm.at[l], psi.at[l]))
        loads.append((lop_hbm.at[:, l], lop.at[:, l]))
    for r in range(nr):
        loads.append((rop_hbm.at[:, r], rop.at[:, r]))
    loads = [pltpu.make_async_copy(src, dst, load.at[i]) for i, (src, dst) in enumerate(loads)]
    for copy in loads:
        copy.start()

    barrier = pltpu.get_barrier_semaphore()
    greeted = [partner, *ring_to.values(), *(final_to(k, steps) for k in range(2) for steps in NEAR)]
    for who in greeted:
        pl.semaphore_signal(barrier, inc=1, device_id=who, device_id_type=MESH)

    sent = []

    def remote(src, dst, n, r, who):
        return pltpu.make_async_remote_copy(
            src_ref=src, dst_ref=dst, send_sem=send.at[r, n], recv_sem=recv.at[r, n], device_id=who, device_id_type=MESH
        )

    def start(copy):
        copy.start()
        sent.append(copy)

    def exchange(r, g):
        slots = pl.ds(GROUPS[g][0], GROUPS[g][1] - GROUPS[g][0])
        return remote(acc.at[r, 1 - core, slots], peer.at[r, slots], g, r, partner)

    def relays(r, stage):
        if stage == 0:
            return ((3, 1, 2), (-3, -1, -2), (4, 2, 2) if r % 2 == 0 else (4, -2, -2))
        return ((2, 1, 1), (-2, -1, -1))

    def relay_copy(r, k, stage, at):
        far, steps, _ = relays(r, stage)[at]
        n = 3 * stage + at
        return remote(acc.at[r, core, SLOT[far], k], ring.at[r, k, n], 2 + k * 5 + n, r, ring_to[steps])

    def start_relays(r, k, stage):
        for at in range(3 - stage):
            start(relay_copy(r, k, stage, at))

    def final_copy(r, k, at):
        far = NEAR[at]
        return remote(acc.at[r, core, SLOT[far], k], final.at[k, at, r], 12 + k * 3 + at, r, final_to(k, far))

    def split_left(g, l):
        first, last = GROUPS[g]
        for t in range(terms):
            for at in range(first, last):
                high, low = split(lop[t, l, (y + FAR[at] + ny) % ny])
                rows = pl.ds((t * (last - first) + at - first) * 16, 16)
                lcat[l, rows, 0:s] = high
                lcat[l, rows, s : 2 * s] = low

    def split_wave(l):
        for r in range(nr):
            high, low = split(psi[l, r])
            for k in range(2):
                pcat[l, r, k * s : (k + 1) * s, 0:s] = high
                pcat[l, r, k * s : (k + 1) * s, s : 2 * s] = low

    def split_right(r):
        for t in range(terms):
            weight = shift[t].astype(F32)
            for k, w in enumerate((weight, 1.0 - weight)):
                high, low = split(rop[t, r] * w)
                rows = pl.ds(k * s, s)
                wcat[r, rows, t * s : (t + 1) * s] = high
                wcat[r, rows, depth + t * s : depth + (t + 1) * s] = high
                wlow[r, rows, t * s : (t + 1) * s] = low

    def first_product(g, l, r):
        first, last = GROUPS[g]
        size = (last - first) * 16
        both = jnp.dot(lcat[l, 0 : terms * size], pcat[l, r], preferred_element_type=F32)
        high, low = split(both[:, 0:s] + both[:, s : 2 * s])
        rows = pl.ds(l * size, size)
        for t in range(terms):
            x[r, rows, t * s : (t + 1) * s] = high[t * size : (t + 1) * size]
            x[r, rows, depth + t * s : depth + (t + 1) * s] = low[t * size : (t + 1) * size]

    def second_product(g, r):
        first, last = GROUPS[g]
        size = (last - first) * 16
        nt = (((1,), (1,)), ((), ()))
        total = lax.dot_general(x[r, 0 : nl * size], wcat[r], nt, preferred_element_type=F32)
        total += lax.dot_general(x[r, 0 : nl * size, 0:depth], wlow[r], nt, preferred_element_type=F32)
        total = total.reshape(nl, last - first, 2, 8, 2 * s)
        for l in range(nl):
            for c in range(2):
                for k in range(2):
                    acc[r, c, first:last, k, l] = total[l, :, c, :, k * s : (k + 1) * s]

    def take_exchange(g, r):
        first, last = GROUPS[g]
        exchange(r, g).wait_recv()
        acc[r, core, first:last] += peer[r, first:last]

    def take_relays(r, k, stage):
        for at in range(3 - stage):
            relay_copy(r, k, stage, at).wait_recv()
        for at in range(3 - stage):
            far = relays(r, stage)[at][2]
            acc[r, core, SLOT[far], k] += ring[r, k, 3 * stage + at]

    for l in range(nl):
        loads[2 * l].wait()
        loads[2 * l + 1].wait()
        split_wave(l)
        split_left(0, l)
        for r in range(nr):
            first_product(0, l, r)
    for r in range(nr):
        loads[2 * nl + r].wait()
        split_right(r)
        second_product(0, r)
        if r == 0:
            pl.semaphore_wait(barrier, len(greeted))
        start(exchange(r, 0))
    for r in range(nr):
        take_exchange(0, r)
        start_relays(r, classes[0], 0)
    for r in range(nr):
        start_relays(r, classes[1], 0)
    for l in range(nl):
        split_left(1, l)
        for r in range(nr):
            first_product(1, l, r)
    for r in range(nr):
        second_product(1, r)
        start(exchange(r, 1))
    for r in range(nr):
        take_exchange(1, r)
        take_relays(r, classes[0], 0)
        start_relays(r, classes[0], 1)
    for r in range(nr):
        take_relays(r, classes[1], 0)
        start_relays(r, classes[1], 1)
    for r in range(nr):
        start(final_copy(r, classes[0], 0))
    for k in classes:
        for r in range(nr):
            take_relays(r, k, 1)
            for at in range(1, 3):
                start(final_copy(r, k, at))
        if k is classes[0]:
            for r in range(nr):
                start(final_copy(r, classes[1], 0))

    up_l = (lsec == 0).astype(jnp.int32)
    up_r = (rsec == n_rsec - 1).astype(jnp.int32)
    down_l = (lsec == n_lsec - 1).astype(jnp.int32)
    down_r = (rsec == 0).astype(jnp.int32)

    def picked(k, l, r):
        inside = (l >= 0) & (l < nl) & (r >= 0) & (r < nr)
        l, r = jnp.clip(l, 0, nl - 1), jnp.clip(r, 0, nr - 1)
        tile = sum(final[k, at, r, l] for at in range(1, len(NEAR))) + final[k, 0, r, l]
        return jnp.where(inside, tile, 0.0)

    for r in range(nr):
        for at in range(len(NEAR)):
            for k in range(2):
                final_copy(r, k, at).wait_recv()
    for l in range(nl):
        for r in range(nr):
            out[l, r] = picked(0, l - up_l, r + up_r) + picked(1, l + down_l, r - down_r)
    for copy in sent:
        copy.wait_send()


def shards(wavefn, left_ops, right_ops, term_shift):
    nl, nr, s = wavefn.shape[:3]
    terms = left_ops.shape[0]
    ny = lax.axis_size("op") // 2
    most = max(last - first for first, last in GROUPS) * 16
    hbm = pl.BlockSpec(memory_space=pl.ANY)
    left_ops = left_ops.reshape(terms, nl, ny, 16, s)
    return pl.pallas_call(
        kernel,
        out_shape=pltpu.VMEM((nl, nr, 8, s), F32),
        in_specs=[pl.BlockSpec(memory_space=pltpu.SMEM), hbm, hbm, hbm],
        out_specs=pl.BlockSpec(memory_space=pltpu.VMEM),
        scratch_shapes=[
            pltpu.VMEM(wavefn.shape, F32),
            pltpu.VMEM(left_ops.shape, F32),
            pltpu.VMEM(right_ops.shape, F32),
            pltpu.VMEM((nl, terms * most, 2 * s), BF16),
            pltpu.VMEM((nl, nr, 2 * s, 2 * s), BF16),
            pltpu.VMEM((nr, 2 * s, 2 * terms * s), BF16),
            pltpu.VMEM((nr, 2 * s, terms * s), BF16),
            pltpu.VMEM((nr, nl * most, 2 * terms * s), BF16),
            pltpu.VMEM((nr, 2, ny, 2, nl, 8, s), F32),
            pltpu.VMEM((nr, ny, 2, nl, 8, s), F32),
            pltpu.VMEM((nr, 2, 5, nl, 8, s), F32),
            pltpu.VMEM((2, len(NEAR), nr, nl, 8, s), F32),
            pltpu.SemaphoreType.DMA((2 * nl + nr,)),
            pltpu.SemaphoreType.DMA((nr, 18)),
            pltpu.SemaphoreType.DMA((nr, 18)),
        ],
        compiler_params=pltpu.CompilerParams(collective_id=0, has_side_effects=True, vmem_limit_bytes=60 * 2**20),
        name="sigma",
    )(term_shift, wavefn, left_ops, right_ops)


def solution(mesh):
    placed = (
        P("lsec", "rsec", None, None),
        P("op", "lsec", None, None),
        P("op", "rsec", None, None),
        P("op"),
    )
    return jax.shard_map(
        shards, mesh=mesh, in_specs=placed, out_specs=P("lsec", "rsec", "op", None), check_vma=False
    )
```
